512 devices in a mesh: patch: 32 (over x, z), lag: 16 (over y, core).
Axes of the slice: x: 4, y: 8, z: 8, core: 2. Of those that a mesh axis runs over, the one named last changes fastest.
Arguments:
- history: bfloat16 [16, 128, 32768], P('lag', None, 'patch'), may hold values from -6 to 6
- coupling: bfloat16 [16, 32768, 1024], P('lag', 'patch'), may hold values from -0.046875 to 0.046875
- inverse: bfloat16 [32768, 1024], P('patch'), may hold values from -0.1875 to 0.1875
- cotangent: bfloat16 [6, 128, 32768], P(None, 'lag', 'patch'), may hold values from -6 to 6
- targets: int32 [16, 32], P('lag'), may hold values from 0 to 31
Outputs:
- adjoint: bfloat16 [6, 128, 32768], P(None, 'lag', 'patch')
The draws below stay inside these ranges and needn't reach their ends.
Inputs may be any that keep to these rules, and one draw needn't show every extreme that they name: `targets`: each lag and source patch lists exactly one target patch; several sources may list the same target.
All inputs are finite; a program needn't handle non-finite values.
Results may differ from the reference program's by a relative error of at most 0.0085.
Values may be sent and summed in bfloat16 or wider, within the bound.
No kernel may reach another device: no remote copies, remote signals or barrier semaphores. Data moves between devices by JAX's collectives and lax.ppermute only.
A program may use at most 64 MiB of HBM per device.

```python
import jax
import jax.numpy as jnp
from jax import lax

U = 1024
R = 128
STEPS = 6
LAGS = 16
PATCHES = 32


def set_ends(drawn, rng, smallest, high):
    index_at = [jax.random.randint(jax.random.fold_in(rng, axis), (), 0, length) for axis, length in enumerate(drawn.shape)]
    longest = drawn.shape.index(max(drawn.shape))
    neighbour = index_at[:longest] + [(index_at[longest] + 1) % drawn.shape[longest]] + index_at[longest + 1:]
    return drawn.at[tuple(index_at)].set(smallest).at[tuple(neighbour)].set(high)


def block_levels(stream_key, extent, cuts, low, largest):
    factor_of = 1.0
    for position, shards_of in cuts:
        steps = jax.random.uniform(jax.random.fold_in(jax.random.fold_in(stream_key, 6), position), (shards_of,), jnp.float32, low / len(cuts), largest / len(cuts))
        factor_of = factor_of * jnp.repeat(jnp.exp(steps), extent[position] // shards_of).reshape((-1,) + (1,) * (len(extent) - 1 - position))
    return factor_of


def gaussian(own_key, dims, width, bound, cuts=(), kind=jnp.bfloat16):
    entries = jax.random.normal(own_key, dims, jnp.float32) * width
    if len(cuts) > 0:
        entries = block_levels(own_key, dims, cuts, -0.22, 0.18) * entries
    return jnp.clip(entries, min=-bound, max=bound).astype(kind)


def setup_inputs(seed: int = 0) -> dict:
    key_of = jax.random.split(jax.random.key(seed), 6)
    history = gaussian(key_of[0], (LAGS, R, PATCHES * U), 1.0, 6.0, ((0, 16), (2, 32)))
    coupling = gaussian(key_of[1], (LAGS, PATCHES * U, U), (U * LAGS) ** -0.5, 0.046875, ((0, 16), (1, 32)))
    inverse = gaussian(key_of[2], (PATCHES * U, U), U ** -0.5, 0.1875, ((0, 32),))
    cotangent = gaussian(key_of[3], (STEPS, R, PATCHES * U), 1.0, 6.0, ((1, 16), (2, 32)))
    targets = set_ends(jax.random.randint(key_of[4], (LAGS, PATCHES), 0, PATCHES), jax.random.fold_in(key_of[4], 1), 0, PATCHES - 1).astype(jnp.int32)
    return dict(history=history, coupling=coupling, inverse=inverse, cotangent=cotangent, targets=targets)


def reference(history, coupling, inverse, cotangent, targets):
    coupling_tiles = coupling.reshape(LAGS, PATCHES, U, U)
    inverses = inverse.reshape(PATCHES, U, U).astype(jnp.float32)
    histories = history.reshape(LAGS, R, PATCHES, U)
    results = []
    for turn_index in range(STEPS):
        def one_lag(running, members):
            earlier, tile_block, target_row = members
            routed = jnp.take(earlier, target_row, axis=1).astype(jnp.float32)
            added = jnp.einsum("rpi,pij->rpj", routed, tile_block.astype(jnp.float32))
            return running + added, None

        start = jnp.zeros((R, PATCHES, U), jnp.float32)
        partial_value, _ = lax.scan(one_lag, start, (histories, coupling_tiles, targets))
        drive = cotangent[turn_index].reshape(R, PATCHES, U).astype(jnp.float32)
        residual = (drive - partial_value).astype(jnp.bfloat16)
        adjoint_now = jnp.einsum("rpi,pij->rpj", residual.astype(jnp.float32), inverses).astype(jnp.bfloat16)
        results.append(adjoint_now.reshape(R, PATCHES * U))
        histories = jnp.concatenate([adjoint_now[None], histories[:-1]], axis=0)
    return jnp.stack(results)
```

```python
import jax
import jax.numpy as jnp
from jax import lax
from jax.sharding import Mesh, PartitionSpec as P

STEPS = 6
PATCH = ("x", "z")
LAG = ("y", "core")
F32, BF16 = jnp.float32, jnp.bfloat16


def swap(value, axes):
    return lax.all_to_all(value, axes, split_axis=0, concat_axis=0, tiled=True)


def shift(value):
    size = lax.axis_size(LAG)
    return lax.ppermute(value, LAG, [(i, i + 1) for i in range(size - 1)])


def dot(a, b):
    return jnp.dot(a, b, preferred_element_type=F32)


def on_device(history, coupling, inverse, cotangent, targets):
    history, tile, target_row = history[0], coupling[0], targets[0]
    patches, lags = lax.axis_size(PATCH), lax.axis_size(LAG)
    rows, width = history.shape
    piece, own, back = rows // patches, rows // lags, STEPS - 1
    core = lax.axis_index("core")
    chips = lags // 2

    spread = [swap(history.reshape(patches, piece, width), PATCH)]
    for _ in range(back):
        spread.append(shift(spread[-1]))

    chunks = swap(tile.reshape(lags, width // lags, width), LAG)
    first = lax.all_gather(chunks[0], LAG, axis=0, tiled=True)
    later = lax.all_gather(chunks[1:back], LAG, axis=0)
    tiles = [first] + [later[:, i].reshape(width, width) for i in range(back - 1)]

    stacked = jnp.stack(spread, axis=1).reshape(patches, STEPS * piece, width)
    routed = swap(jnp.take(stacked, target_row, axis=0), PATCH)
    terms = dot(routed.reshape(-1, width), tile).reshape(chips, 2, STEPS * own, width)

    mine = target_row[lax.axis_index(PATCH)].astype(BF16)
    note = jnp.full((chips, own, width), mine, BF16)
    kept = lax.dynamic_index_in_dim(terms, core, 1, keepdims=False)
    sent = lax.dynamic_index_in_dim(terms, 1 - core, 1, keepdims=False).astype(BF16)
    got = lax.ppermute(jnp.concatenate([sent, note], 1), "core", [(0, 1), (1, 0)])
    both = (kept + got[:, : STEPS * own].astype(F32)).astype(BF16)
    other = got[:, STEPS * own :]
    half = own // 2
    note0 = jnp.where(core == 0, note, other)[:, :half]
    note1 = jnp.where(core == 0, other, note)[:, :half]
    parts = swap(jnp.concatenate([both, note0, note1], 1), "y")
    base = jnp.sum(parts[:, : STEPS * own].astype(F32), axis=0)
    base = base.reshape(2, STEPS, piece, width).transpose(1, 0, 2, 3).reshape(STEPS, own, width)
    listed = parts[:, STEPS * own :: half, 0].reshape(lags).astype(jnp.int32)

    states, results = [], []
    for k in range(STEPS):
        total = base[k]
        for l in range(k, 0, -1):
            chosen = lax.dynamic_index_in_dim(states[k - l], listed[l - 1], 0, keepdims=False)
            total = total + dot(chosen, tiles[l - 1])
        residual = (cotangent[k].astype(F32) - total).astype(BF16)
        adjoint = dot(residual, inverse).astype(BF16)
        results.append(adjoint)
        if k + 1 < STEPS:
            copies = jnp.broadcast_to(adjoint[None], (patches,) + adjoint.shape)
            states.append(swap(copies, PATCH))
    return jnp.stack(results)


def solution(mesh):
    fine = Mesh(mesh.devices.reshape(4, 8, 8, 2), PATCH + LAG)
    placed = (P(LAG, None, PATCH), P(LAG, PATCH, None), P(PATCH, None), P(None, LAG, PATCH), P(LAG, None))
    return jax.shard_map(
        on_device, mesh=fine, in_specs=placed, out_specs=P(None, LAG, PATCH), check_vma=False
    )
```

```python
import jax
import jax.numpy as jnp
from jax import lax
from jax.sharding import Mesh, PartitionSpec as P

STEPS = 6
PATCH = ("x", "z")
LAG = ("y", "core")
F32, BF16 = jnp.float32, jnp.bfloat16


def swap(value, axes):
    return lax.all_to_all(value, axes, split_axis=0, concat_axis=0, tiled=True)


def dot(a, b):
    return jnp.dot(a, b, preferred_element_type=F32)


def on_device(history, coupling, inverse, cotangent, targets):
    history, tile, target_row = history[0], coupling[0], targets[0]
    patches, lags = lax.axis_size(PATCH), lax.axis_size(LAG)
    rows, width = history.shape
    piece, own, back = rows // patches, rows // lags, STEPS - 1
    core = lax.axis_index("core")
    chips = lags // 2

    spread = swap(history.reshape(patches, piece, width), PATCH)
    mine = target_row[lax.axis_index(PATCH)].astype(BF16)
    note = jnp.stack([jnp.full((piece, width), mine, BF16), jnp.zeros((piece, width), BF16)])
    known = lax.all_gather(jnp.concatenate([spread, note]), LAG, axis=0, tiled=True)
    blocks = patches + 2
    listed = known[patches::blocks, 0, 0].astype(jnp.int32)

    _, tile_after = lax.optimization_barrier((spread, tile))
    chunks = swap(tile_after.reshape(lags, width // lags, width), LAG)
    first = lax.all_gather(chunks[0], LAG, axis=0, tiled=True)
    later = lax.all_gather(chunks[1:back], LAG, axis=0)
    tiles = [first] + [later[:, i].reshape(width, width) for i in range(back - 1)]

    lag = lax.axis_index(LAG)
    earlier = lag - jnp.arange(STEPS)
    index = jnp.where(earlier >= 0, earlier * blocks + target_row[:, None], patches + 1)
    chosen = known.at[index].get(mode="promise_in_bounds")
    routed = swap(chosen.reshape(patches, STEPS * piece, width), PATCH)
    terms = dot(routed.reshape(-1, width), tile).reshape(chips, 2, STEPS * own, width)

    kept = lax.dynamic_index_in_dim(terms, core, 1, keepdims=False)
    sent = lax.dynamic_index_in_dim(terms, 1 - core, 1, keepdims=False).astype(BF16)
    got = lax.ppermute(sent, "core", [(0, 1), (1, 0)])
    both = (kept + got.astype(F32)).astype(BF16)
    base = jnp.sum(swap(both, "y").astype(F32), axis=0)
    base = base.reshape(2, STEPS, piece, width).transpose(1, 0, 2, 3).reshape(STEPS, own, width)

    states, results = [], []
    for k in range(STEPS):
        total = base[k]
        for l in range(k, 0, -1):
            chosen = lax.dynamic_index_in_dim(states[k - l], listed[l - 1], 0, keepdims=False)
            total = total + dot(chosen, tiles[l - 1])
        residual = (cotangent[k].astype(F32) - total).astype(BF16)
        adjoint = dot(residual, inverse).astype(BF16)
        results.append(adjoint)
        if k + 1 < STEPS:
            copies = jnp.broadcast_to(adjoint[None], (patches,) + adjoint.shape)
            states.append(swap(copies, PATCH))
    return jnp.stack(results)


def solution(mesh):
    fine = Mesh(mesh.devices.reshape(4, 8, 8, 2), PATCH + LAG)
    placed = (P(LAG, None, PATCH), P(LAG, PATCH, None), P(PATCH, None), P(None, LAG, PATCH), P(LAG, None))
    return jax.shard_map(
        on_device, mesh=fine, in_specs=placed, out_specs=P(None, LAG, PATCH), check_vma=False
    )
```

```python
import jax
import jax.numpy as jnp
from jax import lax
from jax.sharding import Mesh, PartitionSpec as P

STEPS = 6
PATCH = ("x", "z")
LAG = ("y", "core")
F32, BF16 = jnp.float32, jnp.bfloat16


def swap(value, axes):
    return lax.all_to_all(value, axes, split_axis=0, concat_axis=0, tiled=True)


def dot(a, b):
    return jnp.dot(a, b, preferred_element_type=F32)


def on_device(history, coupling, inverse, cotangent, targets):
    history, tile, target_row = history[0], coupling[0], targets[0]
    patches, lags = lax.axis_size(PATCH), lax.axis_size(LAG)
    rows, width = history.shape
    piece, own, back = rows // patches, rows // lags, STEPS - 1
    core, lag = lax.axis_index("core"), lax.axis_index(LAG)
    chips = lags // 2

    spread = swap(history.reshape(patches, piece, width), PATCH)
    mine = target_row[lax.axis_index(PATCH)].astype(BF16)
    note = jnp.stack([jnp.full((piece, width), mine, BF16), jnp.zeros((piece, width), BF16)])
    known = lax.all_gather(jnp.concatenate([spread, note]), LAG, axis=0, tiled=True)
    blocks = patches + 2
    listed = known[patches::blocks, 0, 0].astype(jnp.int32)

    third = 352
    moved1 = lax.ppermute(tile[third : 2 * third], LAG, [(i, i + back) for i in range(back)])
    moved2 = lax.ppermute(tile[width - third :], LAG, [(i, i + 2 * back) for i in range(back)])
    first = swap(spread.at[target_row].get(mode="promise_in_bounds"), PATCH)
    moved1, moved2, _ = lax.optimization_barrier((moved1, moved2, first))
    share = jnp.where(lag < back, tile[:third], jnp.where(lag < 2 * back, moved1, moved2))
    shares = lax.all_gather(share, LAG, axis=0)

    def tile_of(l):
        last = shares[l - 1 + 2 * back][3 * third - width :]
        return jnp.concatenate([shares[l - 1], shares[l - 1 + back], last])

    first = dot(first.reshape(rows, width), tile).astype(BF16)
    total = jnp.sum(swap(first.reshape(lags, own, width), LAG).astype(F32), axis=0)

    def solve(k, total):
        residual = (cotangent[k].astype(F32) - total).astype(BF16)
        return dot(residual, inverse).astype(BF16)

    results = [solve(0, total)]

    earlier = lag - jnp.arange(1, STEPS)
    index = jnp.where(earlier >= 0, earlier * blocks + target_row[:, None], patches + 1)
    chosen = known.at[index].get(mode="promise_in_bounds")
    held = own // piece
    ahead = jnp.broadcast_to(results[0].reshape(1, held, piece, width), (patches, held, piece, width))
    routed = swap(jnp.concatenate([ahead, chosen], axis=1), PATCH)
    states = [routed[:, :held].reshape(patches, own, width)]
    terms = dot(routed[:, held:].reshape(-1, width), tile).reshape(chips, 2, back * own, width)
    kept = lax.dynamic_index_in_dim(terms, core, 1, keepdims=False)
    sent = lax.dynamic_index_in_dim(terms, 1 - core, 1, keepdims=False).astype(BF16)
    got = lax.ppermute(sent, "core", [(0, 1), (1, 0)])
    both = (kept + got.astype(F32)).astype(BF16)
    base = jnp.sum(swap(both, "y").astype(F32), axis=0)
    base = base.reshape(held, back, piece, width).transpose(1, 0, 2, 3).reshape(back, own, width)

    tiles = [tile_of(l) for l in range(1, STEPS)]
    for k in range(1, STEPS):
        total = base[k - 1]
        for l in range(k, 0, -1):
            state = lax.dynamic_index_in_dim(states[k - l], listed[l - 1], 0, keepdims=False)
            total = total + dot(state, tiles[l - 1])
        results.append(solve(k, total))
        if k + 1 < STEPS:
            copies = jnp.broadcast_to(results[k][None], (patches, own, width))
            states.append(swap(copies, PATCH))
    return jnp.stack(results)


def solution(mesh):
    fine = Mesh(mesh.devices.reshape(4, 8, 8, 2), PATCH + LAG)
    placed = (P(LAG, None, PATCH), P(LAG, PATCH, None), P(PATCH, None), P(None, LAG, PATCH), P(LAG, None))

    return jax.shard_map(on_device, mesh=fine, in_specs=placed, out_specs=P(None, LAG, PATCH), check_vma=False)
```

```python
import jax
import jax.numpy as jnp
from jax import lax
from jax.sharding import Mesh, PartitionSpec as P

STEPS = 6
PATCH = ("x", "z")
LAG = ("y", "core")
F32, BF16 = jnp.float32, jnp.bfloat16


def swap(value, axes):
    return lax.all_to_all(value, axes, split_axis=0, concat_axis=0, tiled=True)


def dot(a, b):
    return jnp.dot(a, b, preferred_element_type=F32)


def on_device(history, coupling, inverse, cotangent, targets):
    history, tile, target_row = history[0], coupling[0], targets[0]
    patches, lags = lax.axis_size(PATCH), lax.axis_size(LAG)
    rows, width = history.shape
    piece, own, back = rows // patches, rows // lags, STEPS - 1
    core, lag = lax.axis_index("core"), lax.axis_index(LAG)
    chips = lags // 2

    spread = swap(history.reshape(patches, piece, width), PATCH)
    mine = target_row[lax.axis_index(PATCH)].astype(BF16)
    note = jnp.stack([jnp.full((piece, width), mine, BF16), jnp.zeros((piece, width), BF16)])
    known = lax.all_gather(jnp.concatenate([spread, note]), LAG, axis=0, tiled=True)
    blocks = patches + 2
    listed = known[patches::blocks, 0, 0].astype(jnp.int32)

    third = 352
    moved1 = lax.ppermute(tile[third : 2 * third], LAG, [(i, i + back) for i in range(back)])
    moved2 = lax.ppermute(tile[width - third :], LAG, [(i, i + 2 * back) for i in range(back)])
    first = swap(spread.at[target_row].get(mode="promise_in_bounds"), PATCH)
    first = dot(first.reshape(rows, width), tile).astype(BF16)
    total = jnp.sum(swap(first.reshape(lags, own, width), LAG).astype(F32), axis=0)
    moved1, moved2, _ = lax.optimization_barrier((moved1, moved2, total))
    share = jnp.where(lag < back, tile[:third], jnp.where(lag < 2 * back, moved1, moved2))
    shares = lax.all_gather(share, LAG, axis=0)

    def tile_of(l, after):
        ready, _ = lax.optimization_barrier((shares, after))
        last = ready[l - 1 + 2 * back][3 * third - width :]
        return jnp.concatenate([ready[l - 1], ready[l - 1 + back], last])

    def solve(k, total):
        residual = (cotangent[k].astype(F32) - total).astype(BF16)
        return dot(residual, inverse).astype(BF16)

    results = [solve(0, total)]

    earlier = lag - jnp.arange(1, STEPS)
    index = jnp.where(earlier >= 0, earlier * blocks + target_row[:, None], patches + 1)
    chosen = known.at[index].get(mode="promise_in_bounds")
    held = own // piece
    ahead = jnp.broadcast_to(results[0].reshape(1, held, piece, width), (patches, held, piece, width))
    routed = swap(jnp.concatenate([ahead, chosen], axis=1), PATCH)
    states = [routed[:, :held].reshape(patches, own, width)]
    routed = routed.reshape(chips, 2, -1, STEPS + 1, piece, width)

    def terms(which):
        part = lax.dynamic_index_in_dim(routed, which, 1, keepdims=False)
        return dot(part[:, :, held:].reshape(-1, width), tile).reshape(chips, back * own, width)

    got = lax.ppermute(terms(1 - core).astype(BF16), "core", [(0, 1), (1, 0)])
    both = (terms(core) + got.astype(F32)).astype(BF16)
    parts = swap(both, "y")
    base = jnp.sum(parts.astype(F32), axis=0)
    base = base.reshape(held, back, piece, width).transpose(1, 0, 2, 3).reshape(back, own, width)

    tiles = [tile_of(1, both)]
    for k in range(1, STEPS):
        total = base[k - 1]
        for l in range(k, 0, -1):
            state = lax.dynamic_index_in_dim(states[k - l], listed[l - 1], 0, keepdims=False)
            total = total + dot(state, tiles[l - 1])
        results.append(solve(k, total))
        if k + 1 < STEPS:
            tiles.append(tile_of(k + 1, results[k]))
            copies = jnp.broadcast_to(results[k][None], (patches, own, width))
            states.append(swap(copies, PATCH))
    return jnp.stack(results)


def solution(mesh):
    fine = Mesh(mesh.devices.reshape(4, 8, 8, 2), PATCH + LAG)
    placed = (P(LAG, None, PATCH), P(LAG, PATCH, None), P(PATCH, None), P(None, LAG, PATCH), P(LAG, None))

    return jax.shard_map(on_device, mesh=fine, in_specs=placed, out_specs=P(None, LAG, PATCH), check_vma=False)
```

```python
import jax
import jax.numpy as jnp
from jax import lax
from jax.sharding import Mesh, PartitionSpec as P

STEPS = 6
PATCH = ("x", "z")
LAG = ("y", "core")
F32, BF16 = jnp.float32, jnp.bfloat16


def swap(value, axes):
    return lax.all_to_all(value, axes, split_axis=0, concat_axis=0, tiled=True)


def dot(a, b):
    return jnp.dot(a, b, preferred_element_type=F32)


def on_device(history, coupling, inverse, cotangent, targets):
    history, tile, target_row = history[0], coupling[0], targets[0]
    patches, lags = lax.axis_size(PATCH), lax.axis_size(LAG)
    rows, width = history.shape
    piece, own, back = rows // patches, rows // lags, STEPS - 1
    core, lag = lax.axis_index("core"), lax.axis_index(LAG)
    chips = lags // 2

    spread = swap(history.reshape(patches, piece, width), PATCH)
    mine = target_row[lax.axis_index(PATCH)].astype(BF16)
    note = jnp.stack([jnp.full((piece, width), mine, BF16), jnp.zeros((piece, width), BF16)])
    known = lax.all_gather(jnp.concatenate([spread, note]), LAG, axis=0, tiled=True)
    blocks = patches + 2
    listed = known[patches::blocks, 0, 0].astype(jnp.int32)

    third = 352
    moved1 = lax.ppermute(tile[third : 2 * third], LAG, [(i, i + back) for i in range(back)])
    moved2 = lax.ppermute(tile[width - third :], LAG, [(i, i + 2 * back) for i in range(back)])
    first = swap(spread.at[target_row].get(mode="promise_in_bounds"), PATCH)
    first = dot(first.reshape(rows, width), tile).astype(BF16)
    total = jnp.sum(swap(first.reshape(lags, own, width), LAG).astype(F32), axis=0)

    def solve(k, total):
        residual = (cotangent[k].astype(F32) - total).astype(BF16)
        return dot(residual, inverse).astype(BF16)

    results = [solve(0, total)]

    moved1, moved2, _ = lax.optimization_barrier((moved1, moved2, results[0]))
    share = jnp.where(lag < back, tile[:third], jnp.where(lag < 2 * back, moved1, moved2))
    shares = lax.all_gather(share, LAG, axis=0)

    def tile_of(l, after):
        ready, _ = lax.optimization_barrier((shares, after))
        last = ready[l - 1 + 2 * back][3 * third - width :]
        return jnp.concatenate([ready[l - 1], ready[l - 1 + back], last])

    earlier = lag - jnp.arange(1, STEPS)
    index = jnp.where(earlier >= 0, earlier * blocks + target_row[:, None], patches + 1)
    chosen = known.at[index].get(mode="promise_in_bounds")
    held = own // piece
    ahead = jnp.broadcast_to(results[0].reshape(1, held, piece, width), (patches, held, piece, width))
    routed = swap(jnp.concatenate([ahead, chosen], axis=1), PATCH)
    states = [routed[:, :held].reshape(patches, own, width)]
    terms = dot(routed[:, held:].reshape(-1, width), tile).astype(BF16)
    terms = terms.reshape(chips, 2, back * own, width)
    kept = lax.dynamic_index_in_dim(terms, core, 1, keepdims=False)
    sent = lax.dynamic_index_in_dim(terms, 1 - core, 1, keepdims=False)
    got = lax.ppermute(sent, "core", [(0, 1), (1, 0)])
    both = (kept.astype(F32) + got.astype(F32)).astype(BF16)
    parts = swap(both, "y")
    base = jnp.sum(parts.astype(F32), axis=0)
    base = base.reshape(held, back, piece, width).transpose(1, 0, 2, 3).reshape(back, own, width)

    tiles = [tile_of(1, both)]
    for k in range(1, STEPS):
        total = base[k - 1]
        for l in range(k, 0, -1):
            state = lax.dynamic_index_in_dim(states[k - l], listed[l - 1], 0, keepdims=False)
            total = total + dot(state, tiles[l - 1])
        results.append(solve(k, total))
        if k + 1 < STEPS:
            tiles.append(tile_of(k + 1, results[k]))
            copies = jnp.broadcast_to(results[k][None], (patches, own, width))
            states.append(swap(copies, PATCH))
    return jnp.stack(results)


def solution(mesh):
    fine = Mesh(mesh.devices.reshape(4, 8, 8, 2), PATCH + LAG)
    placed = (P(LAG, None, PATCH), P(LAG, PATCH, None), P(PATCH, None), P(None, LAG, PATCH), P(LAG, None))

    return jax.shard_map(on_device, mesh=fine, in_specs=placed, out_specs=P(None, LAG, PATCH), check_vma=False)
```

```python
import jax
import jax.numpy as jnp
from jax import lax
from jax.sharding import Mesh, PartitionSpec as P

STEPS = 6
PATCH = ("x", "z")
LAG = ("y", "core")
F32, BF16 = jnp.float32, jnp.bfloat16


def swap(value, axes):
    return lax.all_to_all(value, axes, split_axis=0, concat_axis=0, tiled=True)


def dot(a, b):
    return jnp.dot(a, b, preferred_element_type=F32)


def on_device(history, coupling, inverse, cotangent, targets):
    history, tile, target_row = history[0], coupling[0], targets[0]
    patches, lags = lax.axis_size(PATCH), lax.axis_size(LAG)
    rows, width = history.shape
    piece, own, back = rows // patches, rows // lags, STEPS - 1
    core, lag = lax.axis_index("core"), lax.axis_index(LAG)
    chips = lags // 2

    spread = swap(history.reshape(patches, piece, width), PATCH)
    mine = target_row[lax.axis_index(PATCH)].astype(BF16)
    note = jnp.stack([jnp.full((piece, width), mine, BF16), jnp.zeros((piece, width), BF16)])
    known = lax.all_gather(jnp.concatenate([spread, note]), LAG, axis=0, tiled=True)
    blocks = patches + 2
    listed = known[patches::blocks, 0, 0].astype(jnp.int32)

    third = 352
    moved1 = lax.ppermute(tile[third : 2 * third], LAG, [(i, i + back) for i in range(back)])
    moved2 = lax.ppermute(tile[width - third :], LAG, [(i, i + 2 * back) for i in range(back)])
    first = swap(spread.at[target_row].get(mode="promise_in_bounds"), PATCH)
    first = dot(first.reshape(rows, width), tile).astype(BF16)
    total = jnp.sum(swap(first.reshape(lags, own, width), LAG).astype(F32), axis=0)

    def solve(k, total):
        residual = (cotangent[k].astype(F32) - total).astype(BF16)
        return dot(residual, inverse).astype(BF16)

    results = [solve(0, total)]

    lower = core == 0
    moved1, moved2, lower, _ = lax.optimization_barrier((moved1, moved2, lower, results[0]))
    share = jnp.where(lag < back, tile[:third], jnp.where(lag < 2 * back, moved1, moved2))
    shares = lax.all_gather(share, LAG, axis=0)

    def tile_of(l, after):
        ready, _ = lax.optimization_barrier((shares, after))
        last = ready[l - 1 + 2 * back][3 * third - width :]
        return jnp.concatenate([ready[l - 1], ready[l - 1 + back], last])

    earlier = lag - jnp.arange(1, STEPS)
    index = jnp.where(earlier >= 0, earlier * blocks + target_row[:, None], patches + 1)
    chosen = known.at[index].get(mode="promise_in_bounds")
    held = own // piece
    ahead = jnp.broadcast_to(results[0].reshape(1, held, piece, width), (patches, held, piece, width))
    routed = swap(jnp.concatenate([ahead, chosen], axis=1), PATCH)
    states = [routed[:, :held].reshape(patches, own, width)]
    terms = dot(routed[:, held:].reshape(-1, width), tile).astype(BF16)
    terms = terms.reshape(chips, 2, back * own, width)
    kept = jnp.where(lower, terms[:, 0], terms[:, 1])
    sent = jnp.where(lower, terms[:, 1], terms[:, 0])
    got = lax.ppermute(sent, "core", [(0, 1), (1, 0)])
    both = (kept.astype(F32) + got.astype(F32)).astype(BF16)
    parts = swap(both, "y")
    base = jnp.sum(parts.astype(F32), axis=0)
    base = base.reshape(held, back, piece, width).transpose(1, 0, 2, 3).reshape(back, own, width)

    tiles = [tile_of(1, both)]
    for k in range(1, STEPS):
        total = base[k - 1]
        for l in range(k, 0, -1):
            state = lax.dynamic_index_in_dim(states[k - l], listed[l - 1], 0, keepdims=False)
            total = total + dot(state, tiles[l - 1])
        results.append(solve(k, total))
        if k + 1 < STEPS:
            tiles.append(tile_of(k + 1, results[k - 1]))
            copies = jnp.broadcast_to(results[k][None], (patches, own, width))
            states.append(swap(copies, PATCH))
    return jnp.stack(results)


def solution(mesh):
    fine = Mesh(mesh.devices.reshape(4, 8, 8, 2), PATCH + LAG)
    placed = (P(LAG, None, PATCH), P(LAG, PATCH, None), P(PATCH, None), P(None, LAG, PATCH), P(LAG, None))

    return jax.shard_map(on_device, mesh=fine, in_specs=placed, out_specs=P(None, LAG, PATCH), check_vma=False)
```

```python
import jax
import jax.numpy as jnp
from jax import lax
from jax.sharding import Mesh, PartitionSpec as P

STEPS = 6
PATCH = ("x", "z")
LAG = ("y", "core")
F32, BF16 = jnp.float32, jnp.bfloat16


def swap(value, axes):
    return lax.all_to_all(value, axes, split_axis=0, concat_axis=0, tiled=True)


def dot(a, b):
    return jnp.dot(a, b, preferred_element_type=F32)


def on_device(history, coupling, inverse, cotangent, targets):
    history, tile, target_row = history[0], coupling[0], targets[0]
    patches, lags = lax.axis_size(PATCH), lax.axis_size(LAG)
    rows, width = history.shape
    piece, own, back = rows // patches, rows // lags, STEPS - 1
    core, lag = lax.axis_index("core"), lax.axis_index(LAG)
    chips = lags // 2

    spread = swap(history.reshape(patches, piece, width), PATCH)
    mine = target_row[lax.axis_index(PATCH)].astype(BF16)
    note = jnp.stack([jnp.full((piece, width), mine, BF16), jnp.zeros((piece, width), BF16)])
    known = lax.all_gather(jnp.concatenate([spread, note]), LAG, axis=0, tiled=True)
    blocks = patches + 2
    listed = known[patches::blocks, 0, 0].astype(jnp.int32)

    third = 352
    moved1 = lax.ppermute(tile[third : 2 * third], LAG, [(i, i + back) for i in range(back)])
    moved2 = lax.ppermute(tile[width - third :], LAG, [(i, i + 2 * back) for i in range(back)])
    first = swap(spread.at[target_row].get(mode="promise_in_bounds"), PATCH)
    first = dot(first.reshape(rows, width), tile).astype(BF16)
    total = jnp.sum(swap(first.reshape(lags, own, width), LAG).astype(F32), axis=0)

    def solve(k, total):
        residual = (cotangent[k].astype(F32) - total).astype(BF16)
        return dot(residual, inverse).astype(BF16)

    results = [solve(0, total)]

    lower = core == 0
    moved1, moved2, lower, _ = lax.optimization_barrier((moved1, moved2, lower, results[0]))
    share = jnp.where(lag < back, tile[:third], jnp.where(lag < 2 * back, moved1, moved2))
    shares = lax.all_gather(share, LAG, axis=0)

    def tile_of(l, after):
        ready, _ = lax.optimization_barrier((shares, after))
        last = ready[l - 1 + 2 * back][3 * third - width :]
        return jnp.concatenate([ready[l - 1], ready[l - 1 + back], last])

    earlier = lag - jnp.arange(1, STEPS)
    index = jnp.where(earlier >= 0, earlier * blocks + target_row[:, None], patches + 1)
    chosen = known.at[index].get(mode="promise_in_bounds")
    held = own // piece
    ahead = jnp.broadcast_to(results[0].reshape(1, held, piece, width), (patches, held, piece, width))
    routed = swap(jnp.concatenate([ahead, chosen], axis=1), PATCH)
    states = [routed[:, :held].reshape(patches, own, width)]
    soon, late = held + 2, STEPS + 1

    def terms(rows_of, first, last):
        return dot(rows_of[:, first:last].reshape(-1, width), tile).astype(BF16)

    def per_step(summed, count):
        return list(summed.reshape(held, count, piece, width).transpose(1, 0, 2, 3).reshape(count, own, width))

    near = terms(routed, held, soon).reshape(chips, 2, -1, width)
    kept = jnp.where(lower, near[:, 0], near[:, 1])
    sent = jnp.where(lower, near[:, 1], near[:, 0])
    got = lax.ppermute(sent, "core", [(0, 1), (1, 0)])
    both = (kept.astype(F32) + got.astype(F32)).astype(BF16)
    parts = swap(both, "y")
    base = per_step(jnp.sum(parts.astype(F32), axis=0), 2)
    after, _ = lax.optimization_barrier((routed, sent))
    far = lax.psum_scatter(terms(after, soon, late), LAG, scatter_dimension=0, tiled=True)

    tiles = [tile_of(1, both)]
    for k in range(1, STEPS):
        total = base[k - 1]
        for l in range(k, 0, -1):
            state = lax.dynamic_index_in_dim(states[k - l], listed[l - 1], 0, keepdims=False)
            total = total + dot(state, tiles[l - 1])
        results.append(solve(k, total))
        if k == 2:
            far, _ = lax.optimization_barrier((far, results[k]))
            base += per_step(far.astype(F32), back - 2)
        if k + 1 < STEPS:
            tiles.append(tile_of(k + 1, results[k - 1]))
            copies = jnp.broadcast_to(results[k][None], (patches, own, width))
            states.append(swap(copies, PATCH))
    return jnp.stack(results)


def solution(mesh):
    fine = Mesh(mesh.devices.reshape(4, 8, 8, 2), PATCH + LAG)
    placed = (P(LAG, None, PATCH), P(LAG, PATCH, None), P(PATCH, None), P(None, LAG, PATCH), P(LAG, None))

    return jax.shard_map(on_device, mesh=fine, in_specs=placed, out_specs=P(None, LAG, PATCH), check_vma=False)
```

```python
import jax
import jax.numpy as jnp
from jax import lax
from jax.sharding import Mesh, PartitionSpec as P

STEPS = 6
PATCH = ("x", "z")
LAG = ("y", "core")
F32, BF16 = jnp.float32, jnp.bfloat16


def swap(value, axes):
    return lax.all_to_all(value, axes, split_axis=0, concat_axis=0, tiled=True)


def dot(a, b):
    return jnp.dot(a, b, preferred_element_type=F32)


def on_device(history, coupling, inverse, cotangent, targets):
    history, tile, target_row = history[0], coupling[0], targets[0]
    patches, lags = lax.axis_size(PATCH), lax.axis_size(LAG)
    rows, width = history.shape
    piece, own, back = rows // patches, rows // lags, STEPS - 1
    core, lag = lax.axis_index("core"), lax.axis_index(LAG)
    chips = lags // 2

    spread = swap(history.reshape(patches, piece, width), PATCH)
    mine = target_row[lax.axis_index(PATCH)].astype(BF16)
    note = jnp.stack([jnp.full((piece, width), mine, BF16), jnp.zeros((piece, width), BF16)])
    known = lax.all_gather(jnp.concatenate([spread, note]), LAG, axis=0, tiled=True)
    blocks = patches + 2
    listed = known[patches::blocks, 0, 0].astype(jnp.int32)

    third = 352
    moved1 = lax.ppermute(tile[third : 2 * third], LAG, [(i, i + back) for i in range(back)])
    moved2 = lax.ppermute(tile[width - third :], LAG, [(i, i + 2 * back) for i in range(back)])
    first = swap(spread.at[target_row].get(mode="promise_in_bounds"), PATCH)
    first = dot(first.reshape(rows, width), tile).astype(BF16)
    total = jnp.sum(swap(first.reshape(lags, own, width), LAG).astype(F32), axis=0)

    def solve(k, total):
        residual = (cotangent[k].astype(F32) - total).astype(BF16)
        return dot(residual, inverse).astype(BF16)

    results = [solve(0, total)]

    lower = core == 0
    moved1, moved2, lower, _ = lax.optimization_barrier((moved1, moved2, lower, results[0]))
    share = jnp.where(lag < back, tile[:third], jnp.where(lag < 2 * back, moved1, moved2))
    shares = lax.all_gather(share, LAG, axis=0)

    def tile_of(l, after):
        ready, _ = lax.optimization_barrier((shares, after))
        last = ready[l - 1 + 2 * back][3 * third - width :]
        return jnp.concatenate([ready[l - 1], ready[l - 1 + back], last])

    earlier = lag - jnp.arange(1, STEPS)
    index = jnp.where(earlier >= 0, earlier * blocks + target_row[:, None], patches + 1)
    chosen = known.at[index].get(mode="promise_in_bounds")
    held = own // piece
    ahead = jnp.broadcast_to(results[0].reshape(1, held, piece, width), (patches, held, piece, width))
    routed = swap(jnp.concatenate([ahead, chosen], axis=1), PATCH)
    states = [routed[:, :held].reshape(patches, own, width)]
    count = 3
    soon, late = held + count, STEPS + 1

    def terms(rows_of, first, last):
        return dot(rows_of[:, first:last].reshape(-1, width), tile).astype(BF16)

    def per_step(summed, steps):
        return list(summed.reshape(held, steps, piece, width).transpose(1, 0, 2, 3).reshape(steps, own, width))

    near = terms(routed, held, soon).reshape(chips, 2, -1, width)
    kept = jnp.where(lower, near[:, 0], near[:, 1])
    sent = jnp.where(lower, near[:, 1], near[:, 0])
    got = lax.ppermute(sent, "core", [(0, 1), (1, 0)])
    both = (kept.astype(F32) + got.astype(F32)).astype(BF16)
    parts = swap(both, "y")
    base = per_step(jnp.sum(parts.astype(F32), axis=0), count)

    tiles = [tile_of(1, both)]
    for k in range(1, STEPS):
        total = base[k - 1]
        for l in range(k, 0, -1):
            state = lax.dynamic_index_in_dim(states[k - l], listed[l - 1], 0, keepdims=False)
            total = total + dot(state, tiles[l - 1])
        results.append(solve(k, total))
        if k == 1:
            after, _ = lax.optimization_barrier((routed, results[k]))
            far = terms(after, soon, late)
            far = lax.psum_scatter(far, LAG, scatter_dimension=0, tiled=True)
        if k == count:
            far, _ = lax.optimization_barrier((far, results[k]))
            base += per_step(far.astype(F32), back - count)
        if k + 1 < STEPS:
            tiles.append(tile_of(k + 1, results[k - 1]))
            copies = jnp.broadcast_to(results[k][None], (patches, own, width))
            states.append(swap(copies, PATCH))
    return jnp.stack(results)


def solution(mesh):
    fine = Mesh(mesh.devices.reshape(4, 8, 8, 2), PATCH + LAG)
    placed = (P(LAG, None, PATCH), P(LAG, PATCH, None), P(PATCH, None), P(None, LAG, PATCH), P(LAG, None))

    return jax.shard_map(on_device, mesh=fine, in_specs=placed, out_specs=P(None, LAG, PATCH), check_vma=False)
```

```python
import jax
import jax.numpy as jnp
from jax import lax
from jax.sharding import Mesh, PartitionSpec as P

STEPS = 6
PATCH = ("x", "z")
LAG = ("y", "core")
F32, BF16 = jnp.float32, jnp.bfloat16


def swap(value, axes):
    return lax.all_to_all(value, axes, split_axis=0, concat_axis=0, tiled=True)


def dot(a, b):
    return jnp.dot(a, b, preferred_element_type=F32)


def on_device(history, coupling, inverse, cotangent, targets):
    history, tile, target_row = history[0], coupling[0], targets[0]
    patches, lags = lax.axis_size(PATCH), lax.axis_size(LAG)
    rows, width = history.shape
    piece, own, back = rows // patches, rows // lags, STEPS - 1
    core, lag = lax.axis_index("core"), lax.axis_index(LAG)
    chips = lags // 2

    spread = swap(history.reshape(patches, piece, width), PATCH)
    mine = target_row[lax.axis_index(PATCH)].astype(BF16)
    note = jnp.stack([jnp.full((piece, width), mine, BF16), jnp.zeros((piece, width), BF16)])
    known = lax.all_gather(jnp.concatenate([spread, note]), LAG, axis=0, tiled=True)
    blocks = patches + 2
    listed = known[patches::blocks, 0, 0].astype(jnp.int32)

    third = 352
    moved1 = lax.ppermute(tile[third : 2 * third], LAG, [(i, i + back) for i in range(back)])
    moved2 = lax.ppermute(tile[width - third :], LAG, [(i, i + 2 * back) for i in range(back)])
    first = swap(spread.at[target_row].get(mode="promise_in_bounds"), PATCH)
    first = dot(first.reshape(rows, width), tile).astype(BF16)
    total = jnp.sum(swap(first.reshape(lags, own, width), LAG).astype(F32), axis=0)

    def solve(k, total):
        residual = (cotangent[k].astype(F32) - total).astype(BF16)
        return dot(residual, inverse).astype(BF16)

    results = [solve(0, total)]

    lower = core == 0
    moved1, moved2, lower, _ = lax.optimization_barrier((moved1, moved2, lower, results[0]))
    share = jnp.where(lag < back, tile[:third], jnp.where(lag < 2 * back, moved1, moved2))
    shares = lax.all_gather(share, LAG, axis=0)

    def tile_of(l, after):
        ready, _ = lax.optimization_barrier((shares, after))
        last = ready[l - 1 + 2 * back][3 * third - width :]
        return jnp.concatenate([ready[l - 1], ready[l - 1 + back], last])

    earlier = lag - jnp.arange(1, STEPS)
    index = jnp.where(earlier >= 0, earlier * blocks + target_row[:, None], patches + 1)
    chosen = known.at[index].get(mode="promise_in_bounds")
    held = own // piece
    ahead = jnp.broadcast_to(results[0].reshape(1, held, piece, width), (patches, held, piece, width))
    routed = swap(jnp.concatenate([ahead, chosen], axis=1), PATCH)
    states = [routed[:, :held].reshape(patches, own, width)]
    count = 3
    soon, late = held + count, STEPS + 1

    def terms(rows_of, first, last):
        return dot(rows_of[:, first:last].reshape(-1, width), tile).astype(BF16)

    def per_step(summed, steps):
        return list(summed.reshape(held, steps, piece, width).transpose(1, 0, 2, 3).reshape(steps, own, width))

    near = terms(routed, held, soon).reshape(chips, 2, -1, width)
    kept = jnp.where(lower, near[:, 0], near[:, 1])
    sent = jnp.where(lower, near[:, 1], near[:, 0])
    got = lax.ppermute(sent, "core", [(0, 1), (1, 0)])
    both = (kept.astype(F32) + got.astype(F32)).astype(BF16)
    parts = swap(both, "y")
    base = per_step(jnp.sum(parts.astype(F32), axis=0), count)

    after, _ = lax.optimization_barrier((routed, both))
    far = terms(after, soon, late)
    far = lax.psum_scatter(far, LAG, scatter_dimension=0, tiled=True)

    tiles = [tile_of(1, both)]
    for k in range(1, STEPS):
        def reached(l):
            state = lax.dynamic_index_in_dim(states[k - l], listed[l - 1], 0, keepdims=False)
            return dot(state, tiles[l - 1])

        total = sum(reached(l) for l in range(k, 1, -1))
        if k == count + 1:
            far, _ = lax.optimization_barrier((far, total))
            base += per_step(far.astype(F32), back - count)
        total = base[k - 1] + total + reached(1)
        results.append(solve(k, total))
        if k + 1 < STEPS:
            tiles.append(tile_of(k + 1, results[k - 1]))
            copies = jnp.broadcast_to(results[k][None], (patches, own, width))
            states.append(swap(copies, PATCH))
    return jnp.stack(results)


def solution(mesh):
    fine = Mesh(mesh.devices.reshape(4, 8, 8, 2), PATCH + LAG)
    placed = (P(LAG, None, PATCH), P(LAG, PATCH, None), P(PATCH, None), P(None, LAG, PATCH), P(LAG, None))

    return jax.shard_map(on_device, mesh=fine, in_specs=placed, out_specs=P(None, LAG, PATCH), check_vma=False)
```
